128 devices in a mesh: band: 4 (over z_lo, core), blk: 32 (over x, z_hi, y).
Axes of the slice: x: 4, y: 4, z: 4 (z_hi: 2, z_lo: 2; z = z_hi * 2 + z_lo), core: 2. Of those that a mesh axis runs over, the one named last changes fastest.
Arguments:
- alm: bfloat16 [1024, 12, 16, 2, 1024], P('blk', None, 'band'), may hold values from -6 to 6
- legendre: bfloat16 [1024, 1024, 512], P('blk'), may hold values from -0.005859375 to 0.005859375
- orders: int32 [1024], replicated, may hold values from 0 to 1023, as said below
- data_map: bfloat16 [16, 1024, 2048], P('band', 'blk'), may hold values from -8 to 8
- noise_inv: float32 [16, 1024, 2048], P('band', 'blk'), may hold values from 0.1 to 1
- mixing: bfloat16 [5, 16, 1024, 2048], P(None, 'band', 'blk'), may hold values from -1.5 to 1.5
Outputs:
- components: float32 [12, 5, 1024, 2048], P(None, None, ('blk', 'band'))
The draws below stay inside these ranges and needn't reach their ends.
Inputs may be any that keep to these rules, and one draw needn't show every extreme that they name: Slots 2i and 2i + 1 hold a pair of orders m and 1023 - m; every order from 0 to 1023 stands in exactly one slot.
All inputs are finite; a program needn't handle non-finite values.
Results may differ from the reference program's by a relative error of at most 0.005.
Values may be sent and summed in bfloat16 or wider, within the bound.
A program may use at most 192 MiB of HBM per device.

```python
import math
import jax
import jax.numpy as jnp
from jax import lax

L = 1024
M = 1024
NPHI = 2048
BANDS = 16
COMP = 5
CHAINS = 12
CIRCLES = 1024


def draw_orders(key, part):
    pairs = jax.random.permutation(key, M // 2).astype(jnp.int32)
    slot_index = jnp.arange(M, dtype=jnp.int32)
    first_order = pairs[slot_index // 2]
    return jnp.where(slot_index % 2 == 0, first_order, M - 1 - first_order).astype(jnp.int32)


def block_levels(key, extent, split, least, high):
    def one(position, parts):
        heights = jax.random.uniform(jax.random.fold_in(jax.random.fold_in(key, 6), position), (parts,), jnp.float32, least / len(split), high / len(split))
        return jnp.repeat(jnp.exp(heights), extent[position] // parts).reshape((-1,) + (1,) * (len(extent) - position - 1))

    factor_of = one(*split[0])
    for cut in split[1:]:
        factor_of = factor_of * one(*cut)
    return factor_of


def noise(key, extent, scale, bound, split=(), kind=jnp.bfloat16):
    array = scale * jax.random.normal(key, extent, jnp.float32)
    if split:
        array = array * block_levels(key, extent, split, -0.22, 0.18)
    return jnp.clip(array, -bound, bound).astype(kind)


def setup_inputs(seed: int = 0) -> dict:
    key_list = jax.random.split(jax.random.key(seed), 7)
    return {
        "alm": noise(key_list[0], (M, CHAINS, BANDS, 2, L), 1.0, 6.0, ((0, 32), (2, 4))),
        "legendre": noise(key_list[1], (M, L, CIRCLES // 2), (L * M) ** -0.5, 0.005859375, ((0, 32),)),
        "orders": draw_orders(jax.random.fold_in(key_list[6], 71), 0),
        "data_map": noise(key_list[3], (BANDS, CIRCLES, NPHI), 2.0, 8.0, ((0, 4), (1, 32))),
        "noise_inv": jnp.clip(jnp.exp(math.log(1.0) - 2.3025851 * jax.random.uniform(key_list[4], (BANDS, CIRCLES, NPHI), jnp.float32) ** block_levels(key_list[4], (BANDS, CIRCLES, NPHI), ((0, 4), (1, 32)), -0.2, 0.2)), 0.1, 1.0),
        "mixing": noise(key_list[5], (COMP, BANDS, CIRCLES, NPHI), BANDS ** -0.5, 1.5, ((1, 4), (2, 32))),
    }


def dft_basis(orders, nphi):
    longitude = jnp.arange(nphi, dtype=jnp.int32)
    phase_index = (orders[:, None] * longitude[None, :]) % nphi
    angles = (2.0 * math.pi / nphi) * phase_index.astype(jnp.float32)
    weights = jnp.where(orders == 0, 1.0, 2.0).astype(jnp.float32)[:, None]
    return jnp.stack([weights * jnp.cos(angles), -weights * jnp.sin(angles)], axis=1).astype(jnp.bfloat16)


def reference(alm, legendre, orders, data_map, noise_inv, mixing):
    degree = jnp.arange(L, dtype=jnp.int32)
    sign_table = (1 - 2 * ((degree[None, :] + orders[:, None]) % 2)).astype(jnp.float32)

    def synthesise(operands):
        coefficients, table, sign_row = operands
        wide_coeff = coefficients.astype(jnp.float32)
        wide_table = table.astype(jnp.float32)
        north_part = jnp.einsum("cbjl,lr->cbjr", wide_coeff, wide_table)
        south_part = jnp.einsum("cbjl,lr->cbjr", wide_coeff * sign_row, wide_table)
        circle_values = jnp.concatenate([north_part, south_part[..., ::-1]], axis=-1)
        return circle_values.astype(jnp.bfloat16)

    spectra = lax.map(synthesise, (alm, legendre, sign_table))
    spectra = jnp.moveaxis(spectra, 1, 0)
    basis_table = dft_basis(orders, NPHI).astype(jnp.float32)
    wide_mixing = mixing.astype(jnp.float32)
    data_wide = data_map.astype(jnp.float32)

    def one_chain(chain_spec):
        sky_map = jnp.einsum("mbjr,mjp->brp", chain_spec.astype(jnp.float32), basis_table)
        weighted = (noise_inv * (data_wide - sky_map)).astype(jnp.bfloat16)
        return jnp.einsum("kbrp,brp->krp", wide_mixing, weighted.astype(jnp.float32))

    return lax.map(one_chain, spectra)
```

```python
import functools
import math

import jax
import jax.numpy as jnp
from jax import lax
from jax.experimental import pallas as pl
from jax.experimental.pallas import tpu as pltpu
from jax.sharding import PartitionSpec as P

MESH = pl.DeviceIdType.MESH
BF16 = jnp.bfloat16
F32 = jnp.float32

SLOTS = 32
ROWS = 96
CHAINS = 12
DEG = 1024
NORTH = 512
NPHI = 2048
PAIRS = 6
DEVS = 128
OWN = 8
LEG_BUFS = 3
NTILE = 512
MULT = 37


def chip_position():
    band = lax.axis_index("band")
    blk = lax.axis_index("blk")
    return blk // 8, ((blk // 4) % 2) * 2 + band // 2, blk % 4, band % 2


def peer(step):
    offset = (step * MULT) % DEVS
    x, z, y, core = chip_position()
    px = (x + offset // 32) % 4
    pz = (z + (offset // 8) % 4) % 4
    py = (y + (offset // 2) % 4) % 4
    pc = (core + offset % 2) % 2
    return px * 8 + (pz // 2) * 4 + py, (pz % 2) * 2 + pc


def kernel(
    orders_ref, alm_ref, leg_ref, data_ref, noise_ref, mix_ref, cb_ref, sb_ref, ca_ref, sa_ref,
    out_ref,
    alm_v, leg_v, spec_v, send_v, recv_v, basis_v, lhs_v, sky_v, flip_v, data_v, noise_v, mix_v, stage_v,
    alm_sem, leg_sem, send_sem, recv_sem, in_send_sem, in_recv_sem, out_sem,
):
    band = lax.axis_index("band")
    blk = lax.axis_index("blk")

    def load(s):
        slot = s % LEG_BUFS
        return (
            pltpu.make_async_copy(alm_ref.at[s], alm_v.at[slot], alm_sem.at[slot]),
            pltpu.make_async_copy(leg_ref.at[s], leg_v.at[slot], leg_sem.at[slot]),
        )

    for s in range(LEG_BUFS - 1):
        for copy in load(s):
            copy.start()

    barrier = pltpu.get_barrier_semaphore()

    @pl.loop(1, DEVS)
    def _(step):
        pblk, pband = peer(step)
        pl.semaphore_signal(barrier, inc=1, device_id={"blk": pblk, "band": pband}, device_id_type=MESH)

    row = lax.broadcasted_iota(jnp.int32, (256, 256), 0)
    col = lax.broadcasted_iota(jnp.int32, (256, 256), 1)
    flip_v[0] = jnp.where(row == col, 1.0, 0.0).astype(BF16)
    flip_v[1] = jnp.where(row + col == 255, 1.0, 0.0).astype(BF16)
    lane = lax.broadcasted_iota(jnp.int32, (1, DEG), 1)
    alternate = (1 - 2 * (lane % 2)).astype(F32).astype(BF16)

    def synthesise(s):
        slot = s % LEG_BUFS
        for copy in load(s):
            copy.wait()

        @pl.when(s + LEG_BUFS - 1 < SLOTS)
        def _():
            for copy in load(s + LEG_BUFS - 1):
                copy.start()

        coeff = alm_v[slot]
        both = jnp.concatenate([coeff, coeff * alternate], axis=0)
        values = jnp.dot(both, leg_v[slot], preferred_element_type=F32)
        parity = (1 - 2 * (orders_ref[blk * SLOTS + s] % 2)).astype(F32)
        south = values[ROWS:] * parity
        for c in range(CHAINS):
            where = pl.ds(s, 8, stride=SLOTS)
            for t in range(4):
                lanes = slice(t * 128, t * 128 + 128)
                spec_v[c, t, where] = values[c * 8 : c * 8 + 8, lanes]
                spec_v[c, 4 + t, where] = south[c * 8 : c * 8 + 8, lanes]

    @pl.loop(0, 4)
    def _(s):
        synthesise(s)

    pl.semaphore_wait(barrier, DEVS - 1)

    in_copies = []
    mine = pl.ds(pl.multiple_of(band * 4, 4), 4)
    for hop in range(1, 4):
        other = (band + hop) % 4
        rows = pl.ds(pl.multiple_of(other * OWN, OWN), OWN)
        views = (
            (data_ref.at[:, rows], data_v.at[mine]),
            (noise_ref.at[:, rows], noise_v.at[mine]),
            (mix_ref.at[:, :, rows], mix_v.at[:, mine]),
        )
        for n, (src, dst) in enumerate(views):
            copy = pltpu.make_async_remote_copy(
                src_ref=src, dst_ref=dst, send_sem=in_send_sem.at[hop - 1, n], recv_sem=in_recv_sem.at[n],
                device_id={"band": other}, device_id_type=MESH,
            )
            copy.start()
            in_copies.append(copy)
    own_rows = pl.ds(pl.multiple_of(band * OWN, OWN), OWN)
    pltpu.make_async_copy(data_ref.at[:, own_rows], data_v.at[mine], in_recv_sem.at[0]).start()
    pltpu.make_async_copy(noise_ref.at[:, own_rows], noise_v.at[mine], in_recv_sem.at[1]).start()
    pltpu.make_async_copy(mix_ref.at[:, :, own_rows], mix_v.at[:, mine], in_recv_sem.at[2]).start()

    @pl.loop(4, SLOTS)
    def _(s):
        synthesise(s)

    def turn(i):
        for block in range(4):
            source = block if block < 2 else 5 - block
            parts = []
            for c2 in range(2):
                chain = 2 * i + c2
                tile = jnp.concatenate([spec_v[chain, 2 * source], spec_v[chain, 2 * source + 1]], axis=1).astype(BF16)
                turned = lax.dot_general(
                    flip_v[block // 2], tile, (((1,), (1,)), ((), ())), preferred_element_type=F32
                )
                parts.append(turned.reshape(32, OWN, 256))
            send_v[i, block * 32 : block * 32 + 32] = jnp.concatenate(parts, axis=1).astype(BF16)

    def send(i):
        @pl.loop(1, DEVS)
        def _(step):
            pblk, pband = peer(step)
            pltpu.make_async_remote_copy(
                src_ref=send_v.at[i, pblk * 4 + pband], dst_ref=recv_v.at[i, band, blk],
                send_sem=send_sem.at[i], recv_sem=recv_sem.at[i],
                device_id={"blk": pblk, "band": pband}, device_id_type=MESH,
            ).start()

        pltpu.make_async_copy(send_v.at[i, blk * 4 + band], recv_v.at[i, band, blk], recv_sem.at[i]).start()

    turn(0)

    @pl.loop(1, PAIRS)
    def _(i):
        turn(i)
        send(i - 1)

    send(PAIRS - 1)

    @pl.loop(0, 32)
    def _(b):
        rows = pl.ds(pl.multiple_of(b * SLOTS, SLOTS), SLOTS)
        cb, sb = cb_ref[rows], sb_ref[rows]
        ca, sa = ca_ref[rows], sa_ref[rows]
        for a in range(16):
            cosa, sina = ca[:, a : a + 1], sa[:, a : a + 1]
            tile = jnp.concatenate([cosa * cb - sina * sb, -(sina * cb + cosa * sb)], axis=0)
            basis_v[pl.ds(pl.multiple_of(b * 64, 64), 64), a * 128 : a * 128 + 128] = tile.astype(BF16)

    pltpu.make_async_copy(data_v, data_v, in_recv_sem.at[0]).wait()
    pltpu.make_async_copy(noise_v, noise_v, in_recv_sem.at[1]).wait()
    pltpu.make_async_copy(mix_v, mix_v, in_recv_sem.at[2]).wait()

    first_half = lax.broadcasted_iota(jnp.int32, (16, 128), 1) < 64

    def output(i):
        slot = i % 2
        return pltpu.make_async_copy(stage_v.at[slot], out_ref.at[pl.ds(i * 2, 2)], out_sem.at[slot])

    @pl.loop(0, PAIRS)
    def _(i):
        slot = i % 2
        pltpu.make_async_copy(recv_v.at[i], recv_v.at[i], recv_sem.at[i]).wait()

        @pl.loop(0, 4)
        def _(src_band):
            for g in range(16):
                even = recv_v[i, src_band, 2 * g]
                odd = recv_v[i, src_band, 2 * g + 1]
                for t in range(2):
                    a = even[:, t * 128 : t * 128 + 128]
                    b = odd[:, t * 128 : t * 128 + 128]
                    low = jnp.concatenate([a[:, :64], b[:, :64]], axis=1)
                    high = jnp.concatenate([a[:, 64:], b[:, 64:]], axis=1)
                    base = pl.multiple_of(src_band * 64 + t * 32, 32)
                    lhs_v[pl.ds(base, 16), g * 128 : g * 128 + 128] = low
                    lhs_v[pl.ds(base + 16, 16), g * 128 : g * 128 + 128] = high

        @pl.when(i >= 2)
        def _():
            output(i - 2).wait()

        @pl.loop(0, NPHI // NTILE)
        def _(n):
            wide = pl.ds(pl.multiple_of(n * NTILE, NTILE), NTILE)
            sky_v[...] = jnp.dot(lhs_v[...], basis_v[:, wide], preferred_element_type=F32)
            for h in range(NTILE // 256):
                part = pl.ds(pl.multiple_of(n * NTILE + h * 256, 256), 256)
                sums = [jnp.zeros((16, 256), F32) for _ in range(5)]
                for b in range(16):
                    noise = noise_v[b, :, part]
                    data = data_v[b, :, part].astype(F32)
                    sky = sky_v[b * 16 : b * 16 + 16, h * 256 : h * 256 + 256]
                    noise = jnp.concatenate([noise, noise], axis=0)
                    data = jnp.concatenate([data, data], axis=0)
                    weighted = (noise * (data - sky)).astype(BF16).astype(F32)
                    for k in range(5):
                        mix = mix_v[k, b, :, part].astype(F32)
                        sums[k] = sums[k] + jnp.concatenate([mix, mix], axis=0) * weighted
                for k in range(5):
                    for c2 in range(2):
                        stage_v[slot, c2, k, :, part] = sums[k][c2 * 8 : c2 * 8 + 8]

        output(i).start()

    output(PAIRS - 2).wait()
    output(PAIRS - 1).wait()
    for copy in in_copies:
        copy.wait_send()

    @pl.loop(0, PAIRS)
    def _(i):
        sent = send_v.at[i, pl.ds(0, DEVS - 1)]
        pltpu.make_async_copy(sent, sent, send_sem.at[i]).wait()


def per_device(alm, legendre, orders, data_map, noise_inv, mixing):
    step = 2.0 * math.pi / NPHI
    weights = jnp.where(orders == 0, 1.0, 2.0).astype(F32)[:, None]
    fine = step * (orders[:, None] * jnp.arange(128, dtype=jnp.int32)[None] % NPHI).astype(F32)
    coarse = step * (orders[:, None] * (128 * jnp.arange(16, dtype=jnp.int32))[None] % NPHI).astype(F32)
    any_space = pl.BlockSpec(memory_space=pl.ANY)
    vmem = pl.BlockSpec(memory_space=pltpu.VMEM)
    return pl.pallas_call(
        kernel,
        out_shape=jax.ShapeDtypeStruct((CHAINS, 5, OWN, NPHI), F32),
        in_specs=[pl.BlockSpec(memory_space=pltpu.SMEM)] + [any_space] * 5 + [vmem] * 4,
        out_specs=any_space,
        scratch_shapes=[
            pltpu.VMEM((LEG_BUFS, ROWS, DEG), BF16),
            pltpu.VMEM((LEG_BUFS, DEG, NORTH), BF16),
            pltpu.VMEM((CHAINS, 8, 256, 128), F32),
            pltpu.VMEM((PAIRS, DEVS, 16, 256), BF16),
            pltpu.VMEM((PAIRS, 4, 32, 16, 256), BF16),
            pltpu.VMEM((NPHI, NPHI), BF16),
            pltpu.VMEM((256, NPHI), BF16),
            pltpu.VMEM((256, NTILE), F32),
            pltpu.VMEM((2, 256, 256), BF16),
            pltpu.VMEM((16, OWN, NPHI), BF16),
            pltpu.VMEM((16, OWN, NPHI), F32),
            pltpu.VMEM((5, 16, OWN, NPHI), BF16),
            pltpu.VMEM((2, 2, 5, OWN, NPHI), F32),
            pltpu.SemaphoreType.DMA((LEG_BUFS,)),
            pltpu.SemaphoreType.DMA((LEG_BUFS,)),
            pltpu.SemaphoreType.DMA((PAIRS,)),
            pltpu.SemaphoreType.DMA((PAIRS,)),
            pltpu.SemaphoreType.DMA((3, 3)),
            pltpu.SemaphoreType.DMA((3,)),
            pltpu.SemaphoreType.DMA((2,)),
        ],
        compiler_params=pltpu.CompilerParams(
            collective_id=0, has_side_effects=True, vmem_limit_bytes=63 * 1024 * 1024
        ),
    )(
        orders,
        alm.reshape(SLOTS, ROWS, DEG),
        legendre,
        data_map,
        noise_inv,
        mixing,
        jnp.cos(fine),
        jnp.sin(fine),
        weights * jnp.cos(coarse),
        weights * jnp.sin(coarse),
    )


def solution(mesh):
    placed = (
        P("blk", None, "band", None, None),
        P("blk", None, None),
        P(),
        P("band", "blk", None),
        P("band", "blk", None),
        P(None, "band", "blk", None),
    )
    return jax.shard_map(
        per_device,
        mesh=mesh,
        in_specs=placed,
        out_specs=P(None, None, ("blk", "band"), None),
        check_vma=False,
    )
```
